768 devices in a mesh: mem: 24 (over z, core), reg: 32 (over x, y).
Axes of the slice: x: 4, y: 8, z: 12, core: 2. Of those that a mesh axis runs over, the one named last changes fastest.
Arguments:
- background: bfloat16 [240, 32, 24576], P('mem', 'reg'), may hold values from -6 to 6
- obs_index: int32 [32, 24, 512], P('reg'), may hold values from 0 to 1023
- yobs: bfloat16 [32, 24, 512], P('reg', 'mem'), may hold values from -6 to 6
- loc_list: int32 [32, 24, 2048], P('reg', 'mem'), may hold values from 0 to 4607, as said below
- loc_count: int32 [32, 24], P('reg', 'mem'), may hold values from 256 to 2048, as said below
- loc_weight: float32 [32, 24, 2048], P('reg', 'mem'), may hold values from 0.03 to 0.6
Outputs:
- analysis: bfloat16 [240, 32, 24576], P('mem', 'reg')
The draws below stay inside these ranges and needn't reach their ends.
Inputs may be any that keep to these rules, and one draw needn't show every extreme that they name: `loc_list`: for each region the first loc_count entries name distinct candidates; later entries are candidate numbers that carry no weight. `loc_count`: some region has exactly 2048 entries and some exactly 256.
All inputs are finite; a program needn't handle non-finite values.
Results may differ from the reference program's by a relative error of at most 0.006.
Values may be sent and summed in bfloat16 or wider, within the bound.
No kernel may reach another device: no remote copies, remote signals or barrier semaphores. Data moves between devices by JAX's collectives and lax.ppermute only.
A program may use at most 64 MiB of HBM per device.

```python
import math
import jax
import jax.numpy as jnp
from jax import lax

K = 240
CELLS = 1024
OBS_REG = 512
LMAX = 2048
NS_STEPS = 5
COLS = 32
ROWS = 24


def draw_loc_list(key, part):
    base_key = jax.random.fold_in(key, 11)
    region_keys = jax.random.split(base_key, COLS * ROWS)

    def one_list(subkey):
        return jax.random.permutation(subkey, 9 * OBS_REG)[:LMAX]
    lists = jax.vmap(one_list)(region_keys)
    return lists.reshape(COLS, ROWS, LMAX).astype(jnp.int32)


def draw_loc_count(key, part):
    base_key = jax.random.fold_in(key, 23)
    key_excess, key_top, key_least = jax.random.split(base_key, 3)
    region_total = COLS * ROWS
    least_count = LMAX // 8
    spread_range = LMAX - least_count
    excess = jax.random.randint(key_excess, (region_total,), 0, spread_range + 1)
    counts = least_count + excess * excess // spread_range
    top_position = jax.random.randint(key_top, (), 0, region_total)
    least_position = (top_position + 1 + jax.random.randint(key_least, (), 0, region_total - 1)) % region_total
    positions = jnp.arange(region_total, dtype=jnp.int32)
    counts = jnp.where(positions == top_position, LMAX, counts)
    counts = jnp.where(positions == least_position, least_count, counts)
    return counts.reshape(COLS, ROWS).astype(jnp.int32)


def plant(result, key, low, high):
    spot = [jax.random.randint(jax.random.fold_in(key, axis), (), 0, length) for axis, length in enumerate(result.shape)]
    main_axis = result.shape.index(max(result.shape))
    next_to = spot[:main_axis] + [(spot[main_axis] + 1) % result.shape[main_axis]] + spot[main_axis + 1:]
    return result.at[tuple(spot)].set(low).at[tuple(next_to)].set(high)


def block_levels(key, extent, cuts, least, largest):
    gain = 1.0
    for dim, parts in cuts:
        draws = jax.random.uniform(jax.random.fold_in(jax.random.fold_in(key, 6), dim), (parts,), jnp.float32, least / len(cuts), largest / len(cuts))
        gain = gain * jnp.repeat(jnp.exp(draws), extent[dim] // parts).reshape((-1,) + (1,) * (len(extent) - 1 - dim))
    return gain


def scatter_about(own_key, shape, width, reach, shards=(), held_as=jnp.bfloat16):
    values = jax.random.normal(own_key, shape, jnp.float32) * width
    if len(shards) > 0:
        values = block_levels(own_key, shape, shards, -0.22, 0.18) * values
    return jnp.clip(values, min=-reach, max=reach).astype(held_as)


def setup_inputs(seed: int = 0) -> dict:
    arg_keys = jax.random.split(jax.random.key(seed), 7)
    background = scatter_about(arg_keys[0], (K, COLS, ROWS * CELLS), 1.0, 6.0, ((0, 24), (1, 32)))
    obs_index = plant(jax.random.randint(arg_keys[1], (COLS, ROWS, OBS_REG), 0, CELLS), jax.random.fold_in(arg_keys[1], 1), 0, CELLS - 1).astype(jnp.int32)
    yobs = scatter_about(arg_keys[2], (COLS, ROWS, OBS_REG), 1.0, 6.0, ((0, 32), (1, 24)))
    loc_list = draw_loc_list(jax.random.fold_in(arg_keys[6], 71), 0)
    loc_count = draw_loc_count(jax.random.fold_in(arg_keys[6], 71), 0)
    loc_weight = jnp.clip(jnp.exp(math.log(0.6) - 2.9957323 * jax.random.uniform(arg_keys[5], (COLS, ROWS, LMAX), jnp.float32) ** block_levels(arg_keys[5], (COLS, ROWS, LMAX), ((0, 32), (1, 24)), -0.2, 0.2)), 0.03, 0.6)
    return dict(background=background, obs_index=obs_index, yobs=yobs, loc_list=loc_list, loc_count=loc_count, loc_weight=loc_weight)


inflation = 1.1

def newton_root(gram_matrix):
    size = gram_matrix.shape[0]
    identity = jnp.eye(size, dtype=jnp.float32)
    norm_value = jnp.sqrt(jnp.sum(gram_matrix * gram_matrix))
    current = gram_matrix / norm_value
    inverse_root = identity
    for iteration in range(NS_STEPS):
        correction = 1.5 * identity - 0.5 * jnp.dot(inverse_root, current, precision=lax.Precision.HIGHEST)
        current = jnp.dot(current, correction, precision=lax.Precision.HIGHEST)
        inverse_root = jnp.dot(correction, inverse_root, precision=lax.Precision.HIGHEST)
    return (inverse_root, norm_value)

def analyze(own_state, candidates, obs_order, obs_count, obs_taper):
    members = own_state.shape[0]
    state_mean = lax.optimization_barrier(jnp.sum(own_state.astype(jnp.float32), axis=0)) / members
    state_pert = (own_state.astype(jnp.float32) - state_mean).astype(jnp.bfloat16)
    ensemble = candidates[:members].astype(jnp.float32)
    obs_mean = lax.optimization_barrier(jnp.sum(ensemble, axis=0)) / members
    obs_pert = (ensemble - obs_mean).astype(jnp.bfloat16)
    innovation = (candidates[members].astype(jnp.float32) - obs_mean).astype(jnp.bfloat16)
    local_pert = jnp.take(obs_pert, obs_order, axis=1)
    local_innov = jnp.take(innovation, obs_order)
    positions = jnp.arange(obs_order.shape[0], dtype=jnp.int32)
    live_weight = jnp.where(positions < obs_count, obs_taper, jnp.float32(0.0))
    weighted = (local_pert.astype(jnp.float32) * live_weight).astype(jnp.bfloat16)
    gram_matrix = jnp.dot(weighted, local_pert.T, preferred_element_type=jnp.float32)
    drive_vector = jnp.dot(weighted, local_innov, preferred_element_type=jnp.float32)
    gram_matrix = gram_matrix + (members - 1) / inflation * jnp.eye(members, dtype=jnp.float32)
    inverse_root, norm_value = newton_root(gram_matrix)
    mean_shift = jnp.dot(inverse_root, jnp.dot(inverse_root, drive_vector, precision=lax.Precision.HIGHEST), precision=lax.Precision.HIGHEST)
    weights = math.sqrt(members - 1) / jnp.sqrt(norm_value) * inverse_root + (mean_shift / norm_value)[:, None]
    weights = weights.astype(jnp.bfloat16)
    update = jnp.dot(weights.T, state_pert, preferred_element_type=jnp.float32)
    return (state_mean + update).astype(jnp.bfloat16)

def reference(background, obs_index, yobs, loc_list, loc_count, loc_weight):
    states = background.reshape(K, COLS, ROWS, CELLS)

    def one_region(flat_index):
        column = flat_index // ROWS
        row_index = flat_index % ROWS
        pieces = []
        for offset_col in range(3):
            for offset_row in range(3):
                source_col = (column + offset_col - 1) % COLS
                source_row = (row_index + offset_row - 1) % ROWS
                cells_here = states[:, source_col, source_row, :]
                picked = jnp.take(cells_here, obs_index[source_col, source_row], axis=1)
                pieces.append(jnp.concatenate([picked, yobs[source_col, source_row][None, :]], axis=0))
        candidates = jnp.concatenate(pieces, axis=1)
        return analyze(states[:, column, row_index, :], candidates, loc_list[column, row_index], loc_count[column, row_index], loc_weight[column, row_index])
    regions = lax.map(one_region, jnp.arange(COLS * ROWS, dtype=jnp.int32))
    return regions.reshape(COLS, ROWS, K, CELLS).transpose(2, 0, 1, 3).reshape(K, COLS, ROWS * CELLS)
```

```python
import functools
import math

import jax
import jax.numpy as jnp
from jax import lax
from jax.experimental import pallas as pl
from jax.experimental.pallas import tpu as pltpu
from jax.sharding import PartitionSpec as P

NS_STEPS = 5
INFLATION = 1.1
LANES = 128
VMEM_LIMIT = 24 * 1024 * 1024

F32 = jnp.float32
BF16 = jnp.bfloat16


def call(body, out_shape, scratch=(), flops=0, nbytes=0):
    return pl.pallas_call(
        body,
        out_shape=out_shape,
        scratch_shapes=list(scratch),
        compiler_params=pltpu.CompilerParams(vmem_limit_bytes=VMEM_LIMIT),
        cost_estimate=pl.CostEstimate(flops=flops, bytes_accessed=nbytes, transcendentals=0),
    )


def dot_nn(a, b):
    return lax.dot_general(a, b, (((1,), (0,)), ((), ())), preferred_element_type=F32)


def dot_nt(a, b):
    return lax.dot_general(a, b, (((1,), (1,)), ((), ())), preferred_element_type=F32)


def dot_tn(a, b):
    return lax.dot_general(a, b, (((0,), (0,)), ((), ())), preferred_element_type=F32)


def halves(x):
    high = x.astype(BF16)
    return high, (x - high.astype(F32)).astype(BF16)


def product(a, b):
    return dot_nn(a[0], b[0]) + (dot_nn(a[0], b[1]) + dot_nn(a[1], b[0]))


def pack_kernel(regions, tiles, x_ref, out_ref, wide):
    members = x_ref.shape[0]
    rows = members * tiles
    for q in range(regions):
        for t in range(tiles):
            start = (q * tiles + t) * LANES
            wide[pl.ds(q * rows + t, members, stride=tiles), :] = x_ref[
                :, start : start + LANES
            ].astype(F32)
        out_ref[q] = wide[q * rows : (q + 1) * rows, :].astype(BF16)


def unpack_kernel(regions, tiles, x_ref, out_ref, wide):
    members = out_ref.shape[0]
    rows = members * tiles
    for q in range(regions):
        wide[q * rows : (q + 1) * rows, :] = x_ref[q].astype(F32)
        for t in range(tiles):
            start = (q * tiles + t) * LANES
            out_ref[:, start : start + LANES] = wide[
                pl.ds(q * rows + t, members, stride=tiles), :
            ].astype(BF16)


def weight_kernel(list_ref, count_ref, weight_ref, out_ref):
    length = list_ref.shape[1]
    rows = out_ref.shape[0]
    order = list_ref[...]
    position = lax.broadcasted_iota(jnp.int32, (1, length), 1)
    live = jnp.where(position < count_ref[...], weight_ref[...], 0.0)
    high = live.astype(BF16)
    rest = live - high.astype(F32)
    middle = rest.astype(BF16)
    low = (rest - middle.astype(F32)).astype(BF16)
    row_of = lax.shift_right_logical(order, 7)
    lane_of = lax.bitwise_and(order, 127)
    at_row = lax.broadcasted_iota(jnp.int32, (rows, length), 0) == row_of
    at_lane = lax.broadcasted_iota(jnp.int32, (LANES, length), 0) == lane_of
    lane_hot = jnp.where(at_lane, 1.0, 0.0).astype(BF16)

    def spread(part):
        return dot_nt(jnp.where(at_row, part.astype(F32), 0.0).astype(BF16), lane_hot)

    out_ref[...] = (spread(high) + spread(middle)) + spread(low)


def observe_kernel(tiles, x_ref, index_ref, yobs_ref, out_ref, wide):
    cells = tiles * LANES
    members = x_ref.shape[0] // tiles
    width = index_ref.shape[1]
    wide[...] = x_ref[...].astype(F32)
    index = index_ref[...]
    observed = jnp.zeros((members, width), F32)
    for t in range(tiles):
        cell = lax.broadcasted_iota(jnp.int32, (LANES, width), 0) + t * LANES
        hot = jnp.where(cell == index, 1.0, 0.0).astype(BF16)
        part = wide[pl.ds(t, members, stride=tiles), :].astype(BF16)
        observed = observed + dot_nn(part, hot)
    mean = jnp.sum(observed, axis=0, keepdims=True) / members
    out_ref[:members, :] = (observed - mean).astype(BF16)
    extra = out_ref.shape[0] - members
    innovation = yobs_ref[...].astype(F32) - mean
    row = lax.broadcasted_iota(jnp.int32, (extra, width), 0)
    out_ref[members:, :] = jnp.where(row == 0, innovation, 0.0).astype(BF16)


def state_kernel(tiles, x_ref, mean_ref, pert_ref, wide):
    members = x_ref.shape[0] // tiles
    wide[...] = x_ref[...].astype(F32)
    for t in range(tiles):
        part = wide[pl.ds(t, members, stride=tiles), :]
        mean = jnp.sum(part, axis=0, keepdims=True) / members
        lanes = slice(t * LANES, (t + 1) * LANES)
        mean_ref[:, lanes] = mean
        pert_ref[:, lanes] = (part - mean).astype(BF16)


def gram_kernel(members, before_ref, own_ref, after_ref, w_ref, wl_ref, wr_ref, own_out, left_out, right_out):
    width = own_ref.shape[1]
    chunks = width // LANES
    blocks = (before_ref, own_ref, after_ref)
    per_col = 3 * chunks
    for weights, first, out in (
        (w_ref, per_col, own_out),
        (wl_ref, 0, left_out),
        (wr_ref, 0, right_out),
    ):
        total = None
        for b in range(3):
            rows = blocks[b][...]
            weight = jnp.concatenate(
                [weights[first + b * chunks + c : first + b * chunks + c + 1, :] for c in range(chunks)],
                axis=1,
            )
            weighted = (rows[:members].astype(F32) * weight).astype(BF16)
            term = dot_nt(weighted, rows)
            total = term if total is None else total + term
        out[...] = total


def update_kernel(members, tiles, g_ref, gl_ref, gr_ref, mean_ref, pert_ref, out_ref, wide):
    total = g_ref[...] + (gl_ref[...] + gr_ref[...])
    row = lax.broadcasted_iota(jnp.int32, (members, members), 0)
    col = lax.broadcasted_iota(jnp.int32, (members, members), 1)
    diagonal = row == col
    gram = total[:, :members] + jnp.where(diagonal, (members - 1) / INFLATION, 0.0)
    tail = total.shape[1] - LANES
    drive = total[:, tail:]
    square = jnp.sum(jnp.sum(gram * gram, axis=1, keepdims=True), axis=0, keepdims=True)
    norm = jnp.sqrt(square)

    def correction_of(zy):
        return jnp.where(diagonal, 1.5, 0.0) - 0.5 * zy

    current = gram / norm
    correction = correction_of(current)
    inverse = correction
    for step in range(1, NS_STEPS + 1):
        m = halves(correction)
        if step > 1:
            inverse = product(m, halves(inverse))
        if step == NS_STEPS:
            break
        current = product(halves(current), m)
        correction = correction_of(product(halves(inverse), halves(current)))
    root = halves(inverse)
    shift = product(root, halves(product(root, halves(drive))))
    shift = shift[:, members - tail : members - tail + 1]
    weights = (math.sqrt(members - 1) / jnp.sqrt(norm) * inverse + shift / norm).astype(BF16)
    update = dot_tn(weights, pert_ref[...])
    for t in range(tiles):
        lanes = slice(t * LANES, (t + 1) * LANES)
        wide[pl.ds(t, members, stride=tiles), :] = mean_ref[:, lanes] + update[:, lanes]
    out_ref[...] = wide[...].astype(BF16)


def local(background, obs_index, yobs, loc_list, loc_count, loc_weight):
    share = background.shape[0]
    regions = obs_index.shape[1]
    cells = background.shape[2] // regions
    width = yobs.shape[2]
    tiles = cells // LANES
    members = share * lax.axis_size("mem")
    rows = share * tiles
    padded = members + 16
    chunks = width // LANES
    cand_rows = 9 * chunks

    def ring(axis):
        size = lax.axis_size(axis)
        up = [(i, (i + 1) % size) for i in range(size)]
        return up, [(j, i) for i, j in up]

    mem_up, mem_down = ring("mem")
    reg_up, reg_down = ring("reg")

    weight = call(
        weight_kernel,
        jax.ShapeDtypeStruct((cand_rows, LANES), F32),
        flops=2 * 3 * cand_rows * 2048 * LANES,
        nbytes=1 << 15,
    )(loc_list[0], loc_count, loc_weight[0])
    weight_right = lax.ppermute(weight[: 3 * chunks], "reg", reg_down)
    weight_left = lax.ppermute(weight[6 * chunks :], "reg", reg_up)

    packed = call(
        functools.partial(pack_kernel, regions, tiles),
        jax.ShapeDtypeStruct((regions, rows, LANES), BF16),
        [pltpu.VMEM((regions * rows, LANES), F32)],
        nbytes=2 * 2 * share * regions * cells,
    )(background.reshape(share, regions * cells))
    state = lax.all_to_all(packed, "mem", split_axis=0, concat_axis=0, tiled=True)
    state = state.reshape(members * tiles, LANES)

    own_row = lax.axis_index("mem")
    index = lax.dynamic_slice_in_dim(obs_index[0], own_row, 1, axis=0)
    wide = [pltpu.VMEM((members * tiles, LANES), F32)]
    observed = call(
        functools.partial(observe_kernel, tiles),
        jax.ShapeDtypeStruct((padded, width), BF16),
        wide,
        flops=2 * members * cells * width,
        nbytes=2 * members * cells,
    )(state, index, yobs[0])
    before = lax.ppermute(observed, "mem", mem_up)
    after = lax.ppermute(observed, "mem", mem_down)
    mean, pert = call(
        functools.partial(state_kernel, tiles),
        (
            jax.ShapeDtypeStruct((1, cells), F32),
            jax.ShapeDtypeStruct((members, cells), BF16),
        ),
        wide,
        flops=4 * members * cells,
        nbytes=4 * members * cells,
    )(state)
    gram_shape = jax.ShapeDtypeStruct((members, padded), F32)
    gram, to_left, to_right = call(
        functools.partial(gram_kernel, members),
        (gram_shape,) * 3,
        flops=18 * members * padded * width,
        nbytes=12 * members * padded,
    )(before, observed, after, weight, weight_left, weight_right)
    gram_a = lax.ppermute(to_left, "reg", reg_down)
    gram_b = lax.ppermute(to_right, "reg", reg_up)
    analysis = call(
        functools.partial(update_kernel, members, tiles),
        jax.ShapeDtypeStruct((members * tiles, LANES), BF16),
        wide,
        flops=2 * members * members * (cells + 40 * members),
        nbytes=4 * members * cells,
    )(gram, gram_a, gram_b, mean, pert)
    returned = lax.all_to_all(
        analysis.reshape(regions, rows, LANES), "mem", split_axis=0, concat_axis=0, tiled=True
    )
    out = call(
        functools.partial(unpack_kernel, regions, tiles),
        jax.ShapeDtypeStruct((share, regions * cells), BF16),
        [pltpu.VMEM((regions * rows, LANES), F32)],
        nbytes=2 * 2 * share * regions * cells,
    )(returned)
    return out.reshape(share, 1, regions * cells)


def solution(mesh):
    return jax.shard_map(
        local,
        mesh=mesh,
        in_specs=(
            P("mem", "reg", None),
            P("reg", None, None),
            P("reg", "mem", None),
            P("reg", "mem", None),
            P("reg", "mem"),
            P("reg", "mem", None),
        ),
        out_specs=P("mem", "reg", None),
        check_vma=False,
    )
```

```python
import functools
import math

import jax
import jax.numpy as jnp
from jax import lax
from jax.experimental import pallas as pl
from jax.experimental.pallas import tpu as pltpu
from jax.sharding import PartitionSpec as P

NS_STEPS = 5
INFLATION = 1.1
LANES = 128
VMEM_LIMIT = 24 * 1024 * 1024
PACK_LIMIT = 60 * 1024 * 1024
PIECES = 4

F32 = jnp.float32
BF16 = jnp.bfloat16


def call(body, out_shape, scratch=(), flops=0, nbytes=0, limit=VMEM_LIMIT, **specs):
    return pl.pallas_call(
        body,
        out_shape=out_shape,
        scratch_shapes=list(scratch),
        compiler_params=pltpu.CompilerParams(vmem_limit_bytes=limit),
        cost_estimate=pl.CostEstimate(flops=flops, bytes_accessed=nbytes, transcendentals=0),
        **specs,
    )


def dot_nn(a, b):
    return lax.dot_general(a, b, (((1,), (0,)), ((), ())), preferred_element_type=F32)


def dot_nt(a, b):
    return lax.dot_general(a, b, (((1,), (1,)), ((), ())), preferred_element_type=F32)


def dot_tn(a, b):
    return lax.dot_general(a, b, (((0,), (0,)), ((), ())), preferred_element_type=F32)


def halves(x):
    high = x.astype(BF16)
    return high, (x - high.astype(F32)).astype(BF16)


def product(a, b):
    return dot_nn(jnp.concatenate([a[1], a[0], a[0]], axis=1), jnp.concatenate([b[0], b[1], b[0]], axis=0))


def pack_kernel(regions, tiles, x_hbm, out_hbm, held, wide, made, in_sems, out_sems):
    members = x_hbm.shape[0]
    rows = members * tiles
    group = regions // PIECES
    span = group * tiles * LANES

    def taken(piece):
        lanes = pl.ds(piece * span, span)
        return pltpu.make_async_copy(x_hbm.at[:, lanes], held.at[:, lanes], in_sems.at[piece])

    def given(piece):
        part = pl.ds(piece * group, group)
        return pltpu.make_async_copy(made.at[part], out_hbm.at[part], out_sems.at[piece])

    for piece in range(PIECES):
        taken(piece).start()
    for piece in range(PIECES):
        taken(piece).wait()
        for q in range(piece * group, (piece + 1) * group):
            for t in range(tiles):
                start = (q * tiles + t) * LANES
                wide[pl.ds(q * rows + t, members, stride=tiles), :] = held[
                    :, start : start + LANES
                ].astype(F32)
            made[q] = wide[q * rows : (q + 1) * rows, :].astype(BF16)
        given(piece).start()
    for piece in range(PIECES):
        given(piece).wait()


def unpack_kernel(regions, tiles, x_ref, out_hbm, wide, made, out_sems):
    members = made.shape[0]
    rows = members * tiles
    group = regions // PIECES
    span = group * tiles * LANES

    def given(piece):
        lanes = pl.ds(piece * span, span)
        return pltpu.make_async_copy(made.at[:, lanes], out_hbm.at[:, lanes], out_sems.at[piece])

    for piece in range(PIECES):
        for q in range(piece * group, (piece + 1) * group):
            wide[q * rows : (q + 1) * rows, :] = x_ref[q].astype(F32)
            for t in range(tiles):
                start = (q * tiles + t) * LANES
                made[:, start : start + LANES] = wide[
                    pl.ds(q * rows + t, members, stride=tiles), :
                ].astype(BF16)
        given(piece).start()
    for piece in range(PIECES):
        given(piece).wait()


def weight_kernel(list_ref, count_ref, weight_ref, out_ref):
    length = list_ref.shape[1]
    rows = out_ref.shape[0]
    order = list_ref[...]
    position = lax.broadcasted_iota(jnp.int32, (1, length), 1)
    live = jnp.where(position < count_ref[...], weight_ref[...], 0.0)
    high = live.astype(BF16)
    rest = live - high.astype(F32)
    middle = rest.astype(BF16)
    low = (rest - middle.astype(F32)).astype(BF16)
    row_of = lax.shift_right_logical(order, 7)
    lane_of = lax.bitwise_and(order, 127)
    at_row = lax.broadcasted_iota(jnp.int32, (rows, length), 0) == row_of
    at_lane = lax.broadcasted_iota(jnp.int32, (LANES, length), 0) == lane_of
    lane_hot = jnp.where(at_lane, 1.0, 0.0).astype(BF16)

    def spread(part):
        return dot_nt(jnp.where(at_row, part.astype(F32), 0.0).astype(BF16), lane_hot)

    out_ref[...] = (spread(high) + spread(middle)) + spread(low)


def observe_kernel(tiles, x_ref, index_ref, yobs_ref, wl_ref, wr_ref, out_ref, wide):
    cells = tiles * LANES
    members = x_ref.shape[0] // tiles
    width = index_ref.shape[1]
    wide[...] = x_ref[...].astype(F32)
    index = index_ref[...]
    observed = jnp.zeros((members, width), F32)
    for t in range(tiles):
        cell = lax.broadcasted_iota(jnp.int32, (LANES, width), 0) + t * LANES
        hot = jnp.where(cell == index, 1.0, 0.0).astype(BF16)
        part = wide[pl.ds(t, members, stride=tiles), :].astype(BF16)
        observed = observed + dot_nn(part, hot)
    mean = jnp.sum(observed, axis=0, keepdims=True) / members
    out_ref[:members, :] = (observed - mean).astype(BF16)
    extra = out_ref.shape[0] - members
    innovation = yobs_ref[...].astype(F32) - mean
    row = lax.broadcasted_iota(jnp.int32, (extra, width), 0)
    out_ref[members:, :] = jnp.where(row == 0, innovation, 0.0).astype(BF16)


def packed_gram(members, blocks, w_ref, first):
    chunks = blocks[0].shape[1] // LANES
    total = None
    for b in range(3):
        rows = blocks[b][...]
        start = first + b * chunks
        weight = jnp.concatenate([w_ref[start + c : start + c + 1, :] for c in range(chunks)], axis=1)
        term = dot_nt((rows[:members].astype(F32) * weight).astype(BF16), rows)
        total = term if total is None else total + term
    rest = members - LANES
    row = lax.broadcasted_iota(jnp.int32, (LANES, LANES), 0)
    col = lax.broadcasted_iota(jnp.int32, (LANES, LANES), 1)
    spare = jnp.zeros((LANES - rest, LANES), F32)
    last = jnp.concatenate([total[LANES:, LANES:], spare], axis=0)
    shifted = pltpu.roll(last, LANES - rest, 1)
    upper = jnp.where(row >= col, total[:LANES, :LANES], shifted)
    lower = jnp.where(col == rest + 1, last[:, rest : rest + 1], total[:LANES, LANES:])
    return jnp.concatenate([upper, lower], axis=0)


def unpacked_gram(members, packed):
    rest = members - LANES
    row = lax.broadcasted_iota(jnp.int32, (LANES, LANES), 0)
    col = lax.broadcasted_iota(jnp.int32, (LANES, LANES), 1)
    upper, middle = packed[:LANES], packed[LANES:]
    first = jnp.where(row >= col, upper, 0.0)
    first = first + jnp.where(row > col, upper, 0.0).T
    last = pltpu.roll(upper, rest, 1)
    last = jnp.where((row <= col) & (col < rest), last, 0.0)
    last = last + jnp.where(row < col, last, 0.0).T
    turned = middle.T
    gram = jnp.concatenate(
        [
            jnp.concatenate([first, jnp.where(col < rest, middle, 0.0)], axis=1),
            jnp.concatenate([jnp.where(row < rest, turned, 0.0), last], axis=1),
        ],
        axis=0,
    )
    drive = jnp.concatenate(
        [
            turned[rest : rest + 1],
            jnp.where(col[:1] < rest, turned[rest + 1 : rest + 2], 0.0),
        ],
        axis=1,
    )
    return gram, drive


def neighbour_kernel(members, before_ref, own_ref, after_ref, wl_ref, wr_ref, left_out, right_out):
    blocks = (before_ref, own_ref, after_ref)
    left_out[...] = packed_gram(members, blocks, wl_ref, 0)
    right_out[...] = packed_gram(members, blocks, wr_ref, 0)


def own_kernel(members, tiles, before_ref, own_ref, after_ref, w_ref, x_ref, gram_out, mean_ref, pert_ref, wide):
    gram_out[...] = packed_gram(members, (before_ref, own_ref, after_ref), w_ref, w_ref.shape[0] // 3)
    wide[...] = x_ref[...].astype(F32)
    extra = pert_ref.shape[0] - members
    pert_ref[members:, :] = jnp.zeros((extra, pert_ref.shape[1]), BF16)
    for t in range(tiles):
        part = wide[pl.ds(t, members, stride=tiles), :]
        mean = jnp.sum(part, axis=0, keepdims=True) / members
        lanes = slice(t * LANES, (t + 1) * LANES)
        mean_ref[:, lanes] = mean
        pert_ref[:members, lanes] = (part - mean).astype(BF16)


def update_kernel(members, tiles, g_ref, gl_ref, gr_ref, mean_ref, pert_ref, out_ref, wide):
    gram, drive = unpacked_gram(members, g_ref[...] + (gl_ref[...] + gr_ref[...]))
    size = gram.shape[0]
    row = lax.broadcasted_iota(jnp.int32, (size, size), 0)
    col = lax.broadcasted_iota(jnp.int32, (size, size), 1)
    diagonal = (row == col) & (row < members)
    gram = gram + jnp.where(diagonal, (members - 1) / INFLATION, 0.0)
    square = jnp.sum(jnp.sum(gram * gram, axis=1, keepdims=True), axis=0, keepdims=True)
    norm = jnp.sqrt(square)

    def correction_of(zy):
        return jnp.where(diagonal, 1.5, 0.0) - 0.5 * zy

    current = gram / norm
    correction = correction_of(current)
    moved = jnp.sum(correction * drive, axis=1, keepdims=True)
    inverse = jnp.where(col == members, moved, correction)
    for step in range(1, NS_STEPS + 1):
        m = halves(correction)
        if step > 1:
            inverse = product(m, halves(inverse))
        if step == NS_STEPS:
            break
        current = product(halves(product(halves(current), m)), m)
        correction = correction_of(current)
    shift = jnp.sum(inverse * inverse[:, members : members + 1], axis=0, keepdims=True)
    weights = math.sqrt(members - 1) / jnp.sqrt(norm) * inverse + shift / norm
    weights = weights[:members].astype(BF16)
    update = dot_nn(weights, pert_ref[...])
    for t in range(tiles):
        lanes = slice(t * LANES, (t + 1) * LANES)
        wide[pl.ds(t, members, stride=tiles), :] = mean_ref[:, lanes] + update[:, lanes]
    out_ref[...] = wide[...].astype(BF16)


def local(background, obs_index, yobs, loc_list, loc_count, loc_weight):
    share = background.shape[0]
    regions = obs_index.shape[1]
    cells = background.shape[2] // regions
    width = yobs.shape[2]
    tiles = cells // LANES
    members = share * lax.axis_size("mem")
    rows = share * tiles
    padded = members + 16
    chunks = width // LANES
    cand_rows = 9 * chunks

    def ring(axis):
        size = lax.axis_size(axis)
        up = [(i, (i + 1) % size) for i in range(size)]
        return up, [(j, i) for i, j in up]

    mem_up, mem_down = ring("mem")
    reg_up, reg_down = ring("reg")

    weight = call(
        weight_kernel,
        jax.ShapeDtypeStruct((cand_rows, LANES), F32),
        flops=2 * 3 * cand_rows * 2048 * LANES,
        nbytes=1 << 15,
    )(loc_list[0], loc_count, loc_weight[0])
    weight_right = lax.ppermute(weight[: 3 * chunks], "reg", reg_down)
    weight_left = lax.ppermute(weight[6 * chunks :], "reg", reg_up)

    packed = call(
        functools.partial(pack_kernel, regions, tiles),
        jax.ShapeDtypeStruct((regions, rows, LANES), BF16),
        [
            pltpu.VMEM((share, regions * cells), BF16),
            pltpu.VMEM((regions * rows, LANES), F32),
            pltpu.VMEM((regions, rows, LANES), BF16),
            pltpu.SemaphoreType.DMA((PIECES,)),
            pltpu.SemaphoreType.DMA((PIECES,)),
        ],
        in_specs=[pl.BlockSpec(memory_space=pl.ANY)],
        out_specs=pl.BlockSpec(memory_space=pl.ANY),
        limit=PACK_LIMIT,
        nbytes=2 * 2 * share * regions * cells,
    )(background.reshape(share, regions * cells))
    state = lax.all_to_all(packed, "mem", split_axis=0, concat_axis=0, tiled=True)
    state = state.reshape(members * tiles, LANES)

    own_row = lax.axis_index("mem")
    index = lax.dynamic_slice_in_dim(obs_index[0], own_row, 1, axis=0)
    wide = [pltpu.VMEM((members * tiles, LANES), F32)]
    observed = call(
        functools.partial(observe_kernel, tiles),
        jax.ShapeDtypeStruct((padded, width), BF16),
        wide,
        flops=2 * members * cells * width,
        nbytes=2 * members * cells,
    )(state, index, yobs[0], weight_left, weight_right)
    before = lax.ppermute(observed, "mem", mem_up)
    after = lax.ppermute(observed, "mem", mem_down)
    gram_shape = jax.ShapeDtypeStruct((2 * LANES, LANES), F32)
    to_left, to_right = call(
        functools.partial(neighbour_kernel, members),
        (gram_shape,) * 2,
        flops=12 * members * padded * width,
        nbytes=8 * members * padded,
    )(before, observed, after, weight_left, weight_right)
    gram_a = lax.ppermute(to_left, "reg", reg_down)
    gram_b = lax.ppermute(to_right, "reg", reg_up)
    gram, mean, pert = call(
        functools.partial(own_kernel, members, tiles),
        (
            gram_shape,
            jax.ShapeDtypeStruct((1, cells), F32),
            jax.ShapeDtypeStruct((padded, cells), BF16),
        ),
        wide,
        flops=6 * members * padded * width,
        nbytes=8 * members * cells,
    )(before, observed, after, weight, state)
    analysis = call(
        functools.partial(update_kernel, members, tiles),
        jax.ShapeDtypeStruct((members * tiles, LANES), BF16),
        wide,
        flops=2 * members * members * (cells + 40 * members),
        nbytes=4 * members * cells,
    )(gram, gram_a, gram_b, mean, pert)
    returned = lax.all_to_all(
        analysis.reshape(regions, rows, LANES), "mem", split_axis=0, concat_axis=0, tiled=True
    )
    out = call(
        functools.partial(unpack_kernel, regions, tiles),
        jax.ShapeDtypeStruct((share, regions * cells), BF16),
        [
            pltpu.VMEM((regions * rows, LANES), F32),
            pltpu.VMEM((share, regions * cells), BF16),
            pltpu.SemaphoreType.DMA((PIECES,)),
        ],
        out_specs=pl.BlockSpec(memory_space=pl.ANY),
        nbytes=2 * 2 * share * regions * cells,
    )(returned)
    return out.reshape(share, 1, regions * cells)


def solution(mesh):
    return jax.shard_map(
        local,
        mesh=mesh,
        in_specs=(
            P("mem", "reg", None),
            P("reg", None, None),
            P("reg", "mem", None),
            P("reg", "mem", None),
            P("reg", "mem"),
            P("reg", "mem", None),
        ),
        out_specs=P("mem", "reg", None),
        check_vma=False,
    )
```

```python
import functools
import math

import jax
import jax.numpy as jnp
from jax import lax
from jax.experimental import pallas as pl
from jax.experimental.pallas import tpu as pltpu
from jax.sharding import PartitionSpec as P

NS_STEPS = 5
INFLATION = 1.1
LANES = 128
VMEM_LIMIT = 24 * 1024 * 1024
PACK_LIMIT = 60 * 1024 * 1024
PIECES = 4

F32 = jnp.float32
BF16 = jnp.bfloat16


def call(body, out_shape, scratch=(), flops=0, nbytes=0, limit=VMEM_LIMIT, **specs):
    return pl.pallas_call(
        body,
        out_shape=out_shape,
        scratch_shapes=list(scratch),
        compiler_params=pltpu.CompilerParams(vmem_limit_bytes=limit),
        cost_estimate=pl.CostEstimate(flops=flops, bytes_accessed=nbytes, transcendentals=0),
        **specs,
    )


SCALARS = pl.BlockSpec(memory_space=pltpu.SMEM)
WHOLE = pl.BlockSpec(memory_space=pltpu.VMEM)


def swap(block, axis, place):
    size = lax.axis_size(axis)
    pairs = [(i, (i + 1) % size) for i in range(place, size, 2)]
    return lax.ppermute(block, axis, pairs + [(j, i) for i, j in pairs])


def dot_nn(a, b):
    return lax.dot_general(a, b, (((1,), (0,)), ((), ())), preferred_element_type=F32)


def dot_nt(a, b):
    return lax.dot_general(a, b, (((1,), (1,)), ((), ())), preferred_element_type=F32)


def dot_tn(a, b):
    return lax.dot_general(a, b, (((0,), (0,)), ((), ())), preferred_element_type=F32)


def halves(x):
    high = x.astype(BF16)
    return high, (x - high.astype(F32)).astype(BF16)


def product(a, b):
    return dot_nn(jnp.concatenate([a[1], a[0], a[0]], axis=1), jnp.concatenate([b[0], b[1], b[0]], axis=0))


def pack_kernel(regions, tiles, x_hbm, out_hbm, held, wide, made, in_sems, out_sems):
    members = x_hbm.shape[0]
    rows = members * tiles
    group = regions // PIECES
    span = group * tiles * LANES

    def taken(piece):
        lanes = pl.ds(piece * span, span)
        return pltpu.make_async_copy(x_hbm.at[:, lanes], held.at[:, lanes], in_sems.at[piece])

    def given(piece):
        part = pl.ds(piece * group, group)
        return pltpu.make_async_copy(made.at[part], out_hbm.at[part], out_sems.at[piece])

    for piece in range(PIECES):
        taken(piece).start()
    for piece in range(PIECES):
        taken(piece).wait()
        for q in range(piece * group, (piece + 1) * group):
            for t in range(tiles):
                start = (q * tiles + t) * LANES
                wide[pl.ds(q * rows + t, members, stride=tiles), :] = held[
                    :, start : start + LANES
                ].astype(F32)
            made[q] = wide[q * rows : (q + 1) * rows, :].astype(BF16)
        given(piece).start()
    for piece in range(PIECES):
        given(piece).wait()


def unpack_kernel(regions, tiles, x_ref, out_hbm, wide, made, out_sems):
    members = made.shape[0]
    rows = members * tiles
    group = regions // PIECES
    span = group * tiles * LANES

    def given(piece):
        lanes = pl.ds(piece * span, span)
        return pltpu.make_async_copy(made.at[:, lanes], out_hbm.at[:, lanes], out_sems.at[piece])

    for piece in range(PIECES):
        for q in range(piece * group, (piece + 1) * group):
            wide[q * rows : (q + 1) * rows, :] = x_ref[q].astype(F32)
            for t in range(tiles):
                start = (q * tiles + t) * LANES
                made[:, start : start + LANES] = wide[
                    pl.ds(q * rows + t, members, stride=tiles), :
                ].astype(BF16)
        given(piece).start()
    for piece in range(PIECES):
        given(piece).wait()


def weight_kernel(side_ref, list_ref, count_ref, weight_ref, out_ref, odd_ref, even_ref):
    length = list_ref.shape[1]
    third = out_ref.shape[0]
    rows = 3 * third
    order = list_ref[...]
    position = lax.broadcasted_iota(jnp.int32, (1, length), 1)
    live = jnp.where(position < count_ref[...], weight_ref[...], 0.0)
    high = live.astype(BF16)
    rest = live - high.astype(F32)
    middle = rest.astype(BF16)
    low = (rest - middle.astype(F32)).astype(BF16)
    row_of = lax.shift_right_logical(order, 7)
    lane_of = lax.bitwise_and(order, 127)
    at_row = lax.broadcasted_iota(jnp.int32, (rows, length), 0) == row_of
    at_lane = lax.broadcasted_iota(jnp.int32, (LANES, length), 0) == lane_of
    lane_hot = jnp.where(at_lane, 1.0, 0.0).astype(BF16)

    def spread(part):
        return dot_nt(jnp.where(at_row, part.astype(F32), 0.0).astype(BF16), lane_hot)

    dense = (spread(high) + spread(middle)) + spread(low)
    left, right = dense[:third], dense[2 * third :]
    paired_left = side_ref[1] == 0
    out_ref[...] = dense[third : 2 * third]
    odd_ref[...] = jnp.where(paired_left, left, right)
    even_ref[...] = jnp.where(paired_left, right, left)


def observe_kernel(tiles, x_ref, index_ref, yobs_ref, wo_ref, we_ref, out_ref, wide):
    cells = tiles * LANES
    members = x_ref.shape[0] // tiles
    width = index_ref.shape[1]
    wide[...] = x_ref[...].astype(F32)
    index = index_ref[...]
    observed = jnp.zeros((members, width), F32)
    for t in range(tiles):
        cell = lax.broadcasted_iota(jnp.int32, (LANES, width), 0) + t * LANES
        hot = jnp.where(cell == index, 1.0, 0.0).astype(BF16)
        part = wide[pl.ds(t, members, stride=tiles), :].astype(BF16)
        observed = observed + dot_nn(part, hot)
    mean = jnp.sum(observed, axis=0, keepdims=True) / members
    out_ref[:members, :] = (observed - mean).astype(BF16)
    extra = out_ref.shape[0] - members
    innovation = yobs_ref[...].astype(F32) - mean
    row = lax.broadcasted_iota(jnp.int32, (extra, width), 0)
    out_ref[members:, :] = jnp.where(row == 0, innovation, 0.0).astype(BF16)


def packed_gram(members, side_ref, own_ref, odd_ref, even_ref, w_ref):
    chunks = own_ref.shape[1] // LANES
    side = side_ref[0]
    total = None
    for rows_ref, b in ((own_ref, 1), (odd_ref, 2 * side), (even_ref, 2 - 2 * side)):
        rows = rows_ref[...]
        weight = jnp.concatenate([w_ref[pl.ds(b * chunks + c, 1), :] for c in range(chunks)], axis=1)
        term = dot_nt((rows[:members].astype(F32) * weight).astype(BF16), rows)
        total = term if total is None else total + term
    rest = members - LANES
    row = lax.broadcasted_iota(jnp.int32, (LANES, LANES), 0)
    col = lax.broadcasted_iota(jnp.int32, (LANES, LANES), 1)
    spare = jnp.zeros((LANES - rest, LANES), F32)
    last = jnp.concatenate([total[LANES:, LANES:], spare], axis=0)
    shifted = pltpu.roll(last, LANES - rest, 1)
    upper = jnp.where(row >= col, total[:LANES, :LANES], shifted)
    lower = jnp.where(col == rest + 1, last[:, rest : rest + 1], total[:LANES, LANES:])
    return jnp.concatenate([upper, lower], axis=0)


def unpacked_gram(members, packed):
    rest = members - LANES
    row = lax.broadcasted_iota(jnp.int32, (LANES, LANES), 0)
    col = lax.broadcasted_iota(jnp.int32, (LANES, LANES), 1)
    upper, middle = packed[:LANES], packed[LANES:]
    first = jnp.where(row >= col, upper, 0.0)
    first = first + jnp.where(row > col, upper, 0.0).T
    last = pltpu.roll(upper, rest, 1)
    last = jnp.where((row <= col) & (col < rest), last, 0.0)
    last = last + jnp.where(row < col, last, 0.0).T
    turned = middle.T
    gram = jnp.concatenate(
        [
            jnp.concatenate([first, jnp.where(col < rest, middle, 0.0)], axis=1),
            jnp.concatenate([jnp.where(row < rest, turned, 0.0), last], axis=1),
        ],
        axis=0,
    )
    drive = jnp.concatenate(
        [
            turned[rest : rest + 1],
            jnp.where(col[:1] < rest, turned[rest + 1 : rest + 2], 0.0),
        ],
        axis=1,
    )
    return gram, drive


def neighbour_kernel(members, side_ref, own_ref, odd_ref, even_ref, w_ref, out_ref):
    out_ref[...] = packed_gram(members, side_ref, own_ref, odd_ref, even_ref, w_ref)


def own_kernel(members, tiles, side_ref, own_ref, odd_ref, even_ref, w_ref, x_ref, gram_out, mean_ref, pert_ref, wide):
    gram_out[...] = packed_gram(members, side_ref, own_ref, odd_ref, even_ref, w_ref)
    wide[...] = x_ref[...].astype(F32)
    extra = pert_ref.shape[0] - members
    pert_ref[members:, :] = jnp.zeros((extra, pert_ref.shape[1]), BF16)
    for t in range(tiles):
        part = wide[pl.ds(t, members, stride=tiles), :]
        mean = jnp.sum(part, axis=0, keepdims=True) / members
        lanes = slice(t * LANES, (t + 1) * LANES)
        mean_ref[:, lanes] = mean
        pert_ref[:members, lanes] = (part - mean).astype(BF16)


def update_kernel(members, tiles, g_ref, odd_ref, even_ref, mean_ref, pert_ref, out_ref, wide):
    gram, drive = unpacked_gram(members, g_ref[...] + (odd_ref[...] + even_ref[...]))
    size = gram.shape[0]
    row = lax.broadcasted_iota(jnp.int32, (size, size), 0)
    col = lax.broadcasted_iota(jnp.int32, (size, size), 1)
    diagonal = (row == col) & (row < members)
    gram = gram + jnp.where(diagonal, (members - 1) / INFLATION, 0.0)
    square = jnp.sum(jnp.sum(gram * gram, axis=1, keepdims=True), axis=0, keepdims=True)
    norm = jnp.sqrt(square)

    def correction_of(zy):
        return jnp.where(diagonal, 1.5, 0.0) - 0.5 * zy

    current = gram / norm
    correction = correction_of(current)
    moved = jnp.sum(correction * drive, axis=1, keepdims=True)
    inverse = jnp.where(col == members, moved, correction)
    for step in range(1, NS_STEPS + 1):
        m = halves(correction)
        if step > 1:
            inverse = product(m, halves(inverse))
        if step == NS_STEPS:
            break
        current = product(halves(product(halves(current), m)), m)
        correction = correction_of(current)
    shift = jnp.sum(inverse * inverse[:, members : members + 1], axis=0, keepdims=True)
    weights = math.sqrt(members - 1) / jnp.sqrt(norm) * inverse + shift / norm
    weights = weights[:members].astype(BF16)
    update = dot_nn(weights, pert_ref[...])
    for t in range(tiles):
        lanes = slice(t * LANES, (t + 1) * LANES)
        wide[pl.ds(t, members, stride=tiles), :] = mean_ref[:, lanes] + update[:, lanes]
    out_ref[...] = wide[...].astype(BF16)


def local(background, obs_index, yobs, loc_list, loc_count, loc_weight):
    share = background.shape[0]
    regions = obs_index.shape[1]
    cells = background.shape[2] // regions
    width = yobs.shape[2]
    tiles = cells // LANES
    members = share * lax.axis_size("mem")
    rows = share * tiles
    padded = members + 16
    chunks = width // LANES
    cand_rows = 9 * chunks

    own_row = lax.axis_index("mem")
    side = jnp.stack([own_row % 2, lax.axis_index("reg") % 2]).astype(jnp.int32)
    weight_shape = jax.ShapeDtypeStruct((3 * chunks, LANES), F32)
    weight, weight_odd, weight_even = call(
        weight_kernel,
        (weight_shape,) * 3,
        flops=6 * cand_rows * loc_list.shape[2] * LANES,
        nbytes=1 << 15,
        in_specs=[SCALARS] + [WHOLE] * 3,
    )(side, loc_list[0], loc_count, loc_weight[0])
    weight_odd = swap(weight_odd, "reg", 1)
    weight_even = swap(weight_even, "reg", 0)

    packed = call(
        functools.partial(pack_kernel, regions, tiles),
        jax.ShapeDtypeStruct((regions, rows, LANES), BF16),
        [
            pltpu.VMEM((share, regions * cells), BF16),
            pltpu.VMEM((regions * rows, LANES), F32),
            pltpu.VMEM((regions, rows, LANES), BF16),
            pltpu.SemaphoreType.DMA((PIECES,)),
            pltpu.SemaphoreType.DMA((PIECES,)),
        ],
        in_specs=[pl.BlockSpec(memory_space=pl.ANY)],
        out_specs=pl.BlockSpec(memory_space=pl.ANY),
        limit=PACK_LIMIT,
        nbytes=2 * 2 * share * regions * cells,
    )(background.reshape(share, regions * cells))
    state = lax.all_to_all(packed, "mem", split_axis=0, concat_axis=0, tiled=True)
    state = state.reshape(members * tiles, LANES)

    index = lax.dynamic_slice_in_dim(obs_index[0], own_row, 1, axis=0)
    wide = [pltpu.VMEM((members * tiles, LANES), F32)]
    observed = call(
        functools.partial(observe_kernel, tiles),
        jax.ShapeDtypeStruct((padded, width), BF16),
        wide,
        flops=2 * members * cells * width,
        nbytes=2 * members * cells,
    )(state, index, yobs[0], weight_odd, weight_even)
    rows_in = (side, observed, swap(observed, "mem", 1), swap(observed, "mem", 0))
    gram_shape = jax.ShapeDtypeStruct((2 * LANES, LANES), F32)

    def to_neighbour(place, weights):
        partial = call(
            functools.partial(neighbour_kernel, members),
            gram_shape,
            flops=6 * members * padded * width,
            nbytes=8 * members * padded,
            in_specs=[SCALARS] + [WHOLE] * 4,
        )(*rows_in, weights)
        return swap(partial, "reg", place)

    odd_gram = to_neighbour(1, weight_odd)
    even_gram = to_neighbour(0, weight_even)
    gram, mean, pert = call(
        functools.partial(own_kernel, members, tiles),
        (
            gram_shape,
            jax.ShapeDtypeStruct((1, cells), F32),
            jax.ShapeDtypeStruct((padded, cells), BF16),
        ),
        wide,
        flops=6 * members * padded * width,
        nbytes=8 * members * cells,
        in_specs=[SCALARS] + [WHOLE] * 5,
    )(*rows_in, weight, state)
    analysis = call(
        functools.partial(update_kernel, members, tiles),
        jax.ShapeDtypeStruct((members * tiles, LANES), BF16),
        wide,
        flops=2 * members * members * (cells + 40 * members),
        nbytes=4 * members * cells,
    )(gram, odd_gram, even_gram, mean, pert)
    returned = lax.all_to_all(
        analysis.reshape(regions, rows, LANES), "mem", split_axis=0, concat_axis=0, tiled=True
    )
    out = call(
        functools.partial(unpack_kernel, regions, tiles),
        jax.ShapeDtypeStruct((share, regions * cells), BF16),
        [
            pltpu.VMEM((regions * rows, LANES), F32),
            pltpu.VMEM((share, regions * cells), BF16),
            pltpu.SemaphoreType.DMA((PIECES,)),
        ],
        out_specs=pl.BlockSpec(memory_space=pl.ANY),
        nbytes=2 * 2 * share * regions * cells,
    )(returned)
    return out.reshape(share, 1, regions * cells)


def solution(mesh):
    return jax.shard_map(
        local,
        mesh=mesh,
        in_specs=(
            P("mem", "reg", None),
            P("reg", None, None),
            P("reg", "mem", None),
            P("reg", "mem", None),
            P("reg", "mem"),
            P("reg", "mem", None),
        ),
        out_specs=P("mem", "reg", None),
        check_vma=False,
    )
```

```python
import functools
import math

import jax
import jax.numpy as jnp
from jax import lax
from jax.experimental import pallas as pl
from jax.experimental.pallas import tpu as pltpu
from jax.sharding import PartitionSpec as P

NS_STEPS = 5
INFLATION = 1.1
LANES = 128
VMEM_LIMIT = 24 * 1024 * 1024
PACK_LIMIT = 60 * 1024 * 1024
PIECES = 4

F32 = jnp.float32
BF16 = jnp.bfloat16


def call(body, out_shape, scratch=(), flops=0, nbytes=0, limit=VMEM_LIMIT, **specs):
    return pl.pallas_call(
        body,
        out_shape=out_shape,
        scratch_shapes=list(scratch),
        compiler_params=pltpu.CompilerParams(vmem_limit_bytes=limit),
        cost_estimate=pl.CostEstimate(flops=flops, bytes_accessed=nbytes, transcendentals=0),
        **specs,
    )


SCALARS = pl.BlockSpec(memory_space=pltpu.SMEM)
WHOLE = pl.BlockSpec(memory_space=pltpu.VMEM)


def swap(block, axis, place):
    size = lax.axis_size(axis)
    pairs = [(i, (i + 1) % size) for i in range(place, size, 2)]
    return lax.ppermute(block, axis, pairs + [(j, i) for i, j in pairs])


def dot_nn(a, b):
    return lax.dot_general(a, b, (((1,), (0,)), ((), ())), preferred_element_type=F32)


def dot_nt(a, b):
    return lax.dot_general(a, b, (((1,), (1,)), ((), ())), preferred_element_type=F32)


def dot_tn(a, b):
    return lax.dot_general(a, b, (((0,), (0,)), ((), ())), preferred_element_type=F32)


def halves(x):
    high = x.astype(BF16)
    return high, (x - high.astype(F32)).astype(BF16)


def product(a, b):
    return dot_nn(jnp.concatenate([a[1], a[0], a[0]], axis=1), jnp.concatenate([b[0], b[1], b[0]], axis=0))


def pack_kernel(regions, tiles, x_hbm, out_hbm, held, wide, made, in_sems, out_sems):
    members = x_hbm.shape[0]
    rows = members * tiles
    group = regions // PIECES
    span = group * tiles * LANES

    def taken(piece):
        lanes = pl.ds(piece * span, span)
        return pltpu.make_async_copy(x_hbm.at[:, lanes], held.at[:, lanes], in_sems.at[piece])

    def given(piece):
        part = pl.ds(piece * group, group)
        return pltpu.make_async_copy(made.at[part], out_hbm.at[part], out_sems.at[piece])

    for piece in range(PIECES):
        taken(piece).start()
    for piece in range(PIECES):
        taken(piece).wait()
        for q in range(piece * group, (piece + 1) * group):
            for t in range(tiles):
                start = (q * tiles + t) * LANES
                wide[pl.ds(q * rows + t, members, stride=tiles), :] = held[
                    :, start : start + LANES
                ].astype(F32)
            made[q] = wide[q * rows : (q + 1) * rows, :].astype(BF16)
        given(piece).start()
    for piece in range(PIECES):
        given(piece).wait()


def unpack_kernel(regions, tiles, x_ref, out_hbm, wide, made, out_sems):
    members = made.shape[0]
    rows = members * tiles
    group = regions // PIECES
    span = group * tiles * LANES

    def given(piece):
        lanes = pl.ds(piece * span, span)
        return pltpu.make_async_copy(made.at[:, lanes], out_hbm.at[:, lanes], out_sems.at[piece])

    for piece in range(PIECES):
        for q in range(piece * group, (piece + 1) * group):
            wide[q * rows : (q + 1) * rows, :] = x_ref[q].astype(F32)
            for t in range(tiles):
                start = (q * tiles + t) * LANES
                made[:, start : start + LANES] = wide[
                    pl.ds(q * rows + t, members, stride=tiles), :
                ].astype(BF16)
        given(piece).start()
    for piece in range(PIECES):
        given(piece).wait()


def weight_kernel(side_ref, list_ref, count_ref, weight_ref, out_ref, odd_ref, even_ref):
    length = list_ref.shape[1]
    third = out_ref.shape[0]
    rows = 3 * third
    order = list_ref[...]
    position = lax.broadcasted_iota(jnp.int32, (1, length), 1)
    live = jnp.where(position < count_ref[...], weight_ref[...], 0.0)
    high = live.astype(BF16)
    rest = live - high.astype(F32)
    middle = rest.astype(BF16)
    low = (rest - middle.astype(F32)).astype(BF16)
    row_of = lax.shift_right_logical(order, 7)
    lane_of = lax.bitwise_and(order, 127)
    at_row = lax.broadcasted_iota(jnp.int32, (rows, length), 0) == row_of
    at_lane = lax.broadcasted_iota(jnp.int32, (LANES, length), 0) == lane_of
    lane_hot = jnp.where(at_lane, 1.0, 0.0).astype(BF16)

    def spread(part):
        return dot_nt(jnp.where(at_row, part.astype(F32), 0.0).astype(BF16), lane_hot)

    dense = (spread(high) + spread(middle)) + spread(low)
    left, right = dense[:third], dense[2 * third :]
    paired_left = side_ref[0] == 0
    out_ref[...] = dense[third : 2 * third]
    odd_ref[...] = jnp.where(paired_left, left, right)
    even_ref[...] = jnp.where(paired_left, right, left)


def observe_kernel(tiles, x_ref, index_ref, yobs_ref, wo_ref, we_ref, out_ref, wide):
    cells = tiles * LANES
    members = x_ref.shape[0] // tiles
    width = index_ref.shape[1]
    wide[...] = x_ref[...].astype(F32)
    index = index_ref[...]
    observed = jnp.zeros((members, width), F32)
    for t in range(tiles):
        cell = lax.broadcasted_iota(jnp.int32, (LANES, width), 0) + t * LANES
        hot = jnp.where(cell == index, 1.0, 0.0).astype(BF16)
        part = wide[pl.ds(t, members, stride=tiles), :].astype(BF16)
        observed = observed + dot_nn(part, hot)
    mean = jnp.sum(observed, axis=0, keepdims=True) / members
    out_ref[:members, :] = (observed - mean).astype(BF16)
    extra = out_ref.shape[0] - members
    innovation = yobs_ref[...].astype(F32) - mean
    row = lax.broadcasted_iota(jnp.int32, (extra, width), 0)
    out_ref[members:, :] = jnp.where(row == 0, innovation, 0.0).astype(BF16)


def packed_gram(members, blocks, w_ref):
    chunks = blocks[0].shape[1] // LANES
    total = None
    for b in range(3):
        rows = blocks[b][...]
        start = b * chunks
        weight = jnp.concatenate([w_ref[start + c : start + c + 1, :] for c in range(chunks)], axis=1)
        term = dot_nt((rows[:members].astype(F32) * weight).astype(BF16), rows)
        total = term if total is None else total + term
    rest = members - LANES
    row = lax.broadcasted_iota(jnp.int32, (LANES, LANES), 0)
    col = lax.broadcasted_iota(jnp.int32, (LANES, LANES), 1)
    spare = jnp.zeros((LANES - rest, LANES), F32)
    last = jnp.concatenate([total[LANES:, LANES:], spare], axis=0)
    shifted = pltpu.roll(last, LANES - rest, 1)
    upper = jnp.where(row >= col, total[:LANES, :LANES], shifted)
    lower = jnp.where(col == rest + 1, last[:, rest : rest + 1], total[:LANES, LANES:])
    return jnp.concatenate([upper, lower], axis=0)


def unpacked_gram(members, packed):
    rest = members - LANES
    row = lax.broadcasted_iota(jnp.int32, (LANES, LANES), 0)
    col = lax.broadcasted_iota(jnp.int32, (LANES, LANES), 1)
    upper, middle = packed[:LANES], packed[LANES:]
    first = jnp.where(row >= col, upper, 0.0)
    first = first + jnp.where(row > col, upper, 0.0).T
    last = pltpu.roll(upper, rest, 1)
    last = jnp.where((row <= col) & (col < rest), last, 0.0)
    last = last + jnp.where(row < col, last, 0.0).T
    turned = middle.T
    gram = jnp.concatenate(
        [
            jnp.concatenate([first, jnp.where(col < rest, middle, 0.0)], axis=1),
            jnp.concatenate([jnp.where(row < rest, turned, 0.0), last], axis=1),
        ],
        axis=0,
    )
    drive = jnp.concatenate(
        [
            turned[rest : rest + 1],
            jnp.where(col[:1] < rest, turned[rest + 1 : rest + 2], 0.0),
        ],
        axis=1,
    )
    return gram, drive


def neighbour_kernel(members, before_ref, own_ref, after_ref, wo_ref, we_ref, odd_out, even_out):
    blocks = (before_ref, own_ref, after_ref)
    odd_out[...] = packed_gram(members, blocks, wo_ref)
    even_out[...] = packed_gram(members, blocks, we_ref)


def own_kernel(members, tiles, before_ref, own_ref, after_ref, w_ref, x_ref, gram_out, mean_ref, pert_ref, wide):
    gram_out[...] = packed_gram(members, (before_ref, own_ref, after_ref), w_ref)
    wide[...] = x_ref[...].astype(F32)
    extra = pert_ref.shape[0] - members
    pert_ref[members:, :] = jnp.zeros((extra, pert_ref.shape[1]), BF16)
    for t in range(tiles):
        part = wide[pl.ds(t, members, stride=tiles), :]
        mean = jnp.sum(part, axis=0, keepdims=True) / members
        lanes = slice(t * LANES, (t + 1) * LANES)
        mean_ref[:, lanes] = mean
        pert_ref[:members, lanes] = (part - mean).astype(BF16)


def update_kernel(members, tiles, g_ref, odd_ref, even_ref, mean_ref, pert_ref, out_ref, wide):
    gram, drive = unpacked_gram(members, g_ref[...] + (odd_ref[...] + even_ref[...]))
    size = gram.shape[0]
    row = lax.broadcasted_iota(jnp.int32, (size, size), 0)
    col = lax.broadcasted_iota(jnp.int32, (size, size), 1)
    diagonal = (row == col) & (row < members)
    gram = gram + jnp.where(diagonal, (members - 1) / INFLATION, 0.0)
    square = jnp.sum(jnp.sum(gram * gram, axis=1, keepdims=True), axis=0, keepdims=True)
    norm = jnp.sqrt(square)

    def correction_of(zy):
        return jnp.where(diagonal, 1.5, 0.0) - 0.5 * zy

    current = gram / norm
    correction = correction_of(current)
    moved = jnp.sum(correction * drive, axis=1, keepdims=True)
    inverse = jnp.where(col == members, moved, correction)
    for step in range(1, NS_STEPS + 1):
        m = halves(correction)
        if step > 1:
            inverse = product(m, halves(inverse))
        if step == NS_STEPS:
            break
        current = product(halves(product(halves(current), m)), m)
        correction = correction_of(current)
    shift = jnp.sum(inverse * inverse[:, members : members + 1], axis=0, keepdims=True)
    weights = math.sqrt(members - 1) / jnp.sqrt(norm) * inverse + shift / norm
    weights = weights[:members].astype(BF16)
    update = dot_nn(weights, pert_ref[...])
    for t in range(tiles):
        lanes = slice(t * LANES, (t + 1) * LANES)
        wide[pl.ds(t, members, stride=tiles), :] = mean_ref[:, lanes] + update[:, lanes]
    out_ref[...] = wide[...].astype(BF16)


def local(background, obs_index, yobs, loc_list, loc_count, loc_weight):
    share = background.shape[0]
    regions = obs_index.shape[1]
    cells = background.shape[2] // regions
    width = yobs.shape[2]
    tiles = cells // LANES
    members = share * lax.axis_size("mem")
    rows = share * tiles
    padded = members + 16
    chunks = width // LANES
    cand_rows = 9 * chunks

    side = (lax.axis_index("reg") % 2).astype(jnp.int32).reshape(1)
    weight_shape = jax.ShapeDtypeStruct((3 * chunks, LANES), F32)
    weight, weight_odd, weight_even = call(
        weight_kernel,
        (weight_shape,) * 3,
        flops=6 * cand_rows * loc_list.shape[2] * LANES,
        nbytes=1 << 15,
        in_specs=[SCALARS] + [WHOLE] * 3,
    )(side, loc_list[0], loc_count, loc_weight[0])
    weight_odd = swap(weight_odd, "reg", 1)
    weight_even = swap(weight_even, "reg", 0)

    packed = call(
        functools.partial(pack_kernel, regions, tiles),
        jax.ShapeDtypeStruct((regions, rows, LANES), BF16),
        [
            pltpu.VMEM((share, regions * cells), BF16),
            pltpu.VMEM((regions * rows, LANES), F32),
            pltpu.VMEM((regions, rows, LANES), BF16),
            pltpu.SemaphoreType.DMA((PIECES,)),
            pltpu.SemaphoreType.DMA((PIECES,)),
        ],
        in_specs=[pl.BlockSpec(memory_space=pl.ANY)],
        out_specs=pl.BlockSpec(memory_space=pl.ANY),
        limit=PACK_LIMIT,
        nbytes=2 * 2 * share * regions * cells,
    )(background.reshape(share, regions * cells))
    state = lax.all_to_all(packed, "mem", split_axis=0, concat_axis=0, tiled=True)
    state = state.reshape(members * tiles, LANES)

    index = lax.dynamic_slice_in_dim(obs_index[0], lax.axis_index("mem"), 1, axis=0)
    wide = [pltpu.VMEM((members * tiles, LANES), F32)]
    observed = call(
        functools.partial(observe_kernel, tiles),
        jax.ShapeDtypeStruct((padded, width), BF16),
        wide,
        flops=2 * members * cells * width,
        nbytes=2 * members * cells,
    )(state, index, yobs[0], weight_odd, weight_even)
    size = lax.axis_size("mem")
    up = [(i, (i + 1) % size) for i in range(size)]
    before = lax.ppermute(observed, "mem", up)
    after = lax.ppermute(observed, "mem", [(j, i) for i, j in up])
    rows_in = (before, observed, after)
    gram_shape = jax.ShapeDtypeStruct((2 * LANES, LANES), F32)
    odd_part, even_part = call(
        functools.partial(neighbour_kernel, members),
        (gram_shape,) * 2,
        flops=12 * members * padded * width,
        nbytes=8 * members * padded,
    )(*rows_in, weight_odd, weight_even)
    odd_gram = swap(odd_part, "reg", 1)
    even_gram = swap(even_part, "reg", 0)
    gram, mean, pert = call(
        functools.partial(own_kernel, members, tiles),
        (
            gram_shape,
            jax.ShapeDtypeStruct((1, cells), F32),
            jax.ShapeDtypeStruct((padded, cells), BF16),
        ),
        wide,
        flops=6 * members * padded * width,
        nbytes=8 * members * cells,
    )(*rows_in, weight, state)
    analysis = call(
        functools.partial(update_kernel, members, tiles),
        jax.ShapeDtypeStruct((members * tiles, LANES), BF16),
        wide,
        flops=2 * members * members * (cells + 40 * members),
        nbytes=4 * members * cells,
    )(gram, odd_gram, even_gram, mean, pert)
    returned = lax.all_to_all(
        analysis.reshape(regions, rows, LANES), "mem", split_axis=0, concat_axis=0, tiled=True
    )
    out = call(
        functools.partial(unpack_kernel, regions, tiles),
        jax.ShapeDtypeStruct((share, regions * cells), BF16),
        [
            pltpu.VMEM((regions * rows, LANES), F32),
            pltpu.VMEM((share, regions * cells), BF16),
            pltpu.SemaphoreType.DMA((PIECES,)),
        ],
        out_specs=pl.BlockSpec(memory_space=pl.ANY),
        nbytes=2 * 2 * share * regions * cells,
    )(returned)
    return out.reshape(share, 1, regions * cells)


def solution(mesh):
    return jax.shard_map(
        local,
        mesh=mesh,
        in_specs=(
            P("mem", "reg", None),
            P("reg", None, None),
            P("reg", "mem", None),
            P("reg", "mem", None),
            P("reg", "mem"),
            P("reg", "mem", None),
        ),
        out_specs=P("mem", "reg", None),
        check_vma=False,
    )
```
